128 devices in a mesh: cluster: 16 (over y, x_lo, core), blk: 8 (over x_hi, z).
Axes of the slice: x: 4 (x_hi: 2, x_lo: 2; x = x_hi * 2 + x_lo), y: 4, z: 4, core: 2. Of those that a mesh axis runs over, the one named last changes fastest.
Arguments:
- embeds: bfloat16 [4096, 32, 128], P(('cluster', 'blk')), may hold values from -7 to 7
- labels: int32 [4096, 1], P(('cluster', 'blk')), may hold values from 0 to 15, as said below
- keep: int32 [4096], P(('cluster', 'blk')), may hold values 0 or 1
Outputs:
- dup_score: float32 [4096], P(('cluster', 'blk'))
The draws below stay inside these ranges and needn't reach their ends.
Inputs may be any that keep to these rules, and one draw needn't show every extreme that they name: `labels`: at most 4 prompts of one device carry the same label, and on every device some label is carried by exactly 4 of its prompts.
All inputs are finite; a program needn't handle non-finite values. No bound on the sum of `keep` on one device may be relied on, other than what follows from the above.
Results may differ from the reference program's by a relative error of at most 0.0003.
Values may be sent and summed in bfloat16 or wider, within the bound.
A program may use at most 64 MiB of HBM per device.

```python
import jax
import jax.numpy as jnp
from jax import lax

DIM = 128
TOKS = 32
SLOTS = 64
P_DEV = 32
CLUSTERS = 16
LOOP = 8
CAP = 4
PROMPTS = 4096
N_CLUSTER = 16
N_BLK = 8


def drawn_labels(key):
    key_pop, key_hot, key_rank, key_order = jax.random.split(jax.random.fold_in(key, 7), 4)
    shards = CLUSTERS * LOOP
    popularity = jax.random.randint(key_pop, (CLUSTERS,), 0, 4)
    hottest = jax.random.randint(key_hot, (shards,), 0, CLUSTERS)
    entry_label = (jnp.arange(SLOTS, dtype=jnp.int32) // CAP).astype(jnp.int32)
    tier = popularity[entry_label][None, :] + 8 * (entry_label[None, :] == hottest[:, None]).astype(jnp.int32)
    jitter = jax.random.randint(key_rank, (shards, SLOTS), 0, 4096)
    priority = (tier * 4096 + jitter) * SLOTS + jnp.arange(SLOTS, dtype=jnp.int32)[None, :]
    ranking = jnp.argsort(-priority, axis=1)
    chosen = entry_label[ranking[:, :P_DEV]]
    mixing = jax.random.randint(key_order, (shards, P_DEV), 0, 1 << 20) * P_DEV + jnp.arange(P_DEV, dtype=jnp.int32)[None, :]
    shuffle = jnp.argsort(mixing, axis=1)
    return jnp.take_along_axis(chosen, shuffle, axis=1).reshape(PROMPTS).astype(jnp.int32)


def draw_labels(key, part):
    return drawn_labels(key)[:, None].astype(jnp.int32)


def draw_embeds(key, part):
    label_list = drawn_labels(key)
    keys = jax.random.split(jax.random.fold_in(key, 19), 10)
    families = max(2, P_DEV * LOOP // 5)
    replace_of = 8
    level_lo = 0.1
    level_hi = 0.5
    first_pick = jax.random.randint(keys[0], (PROMPTS,), 0, families)
    second_pick = jax.random.randint(keys[1], (PROMPTS,), 0, families)
    family = jnp.minimum(first_pick, second_pick)
    template_id = label_list * families + family
    templates = jnp.clip(jax.random.normal(keys[2], (CLUSTERS * families, TOKS, DIM), jnp.float32), -4.5, 4.5)
    fresh = jnp.clip(jax.random.normal(keys[3], (PROMPTS, TOKS, DIM), jnp.float32), -4.5, 4.5)
    topic = jnp.clip(jax.random.normal(keys[4], (CLUSTERS, 1, DIM), jnp.float32), -4.5, 4.5)
    base = templates[template_id]
    order_keys = jax.random.randint(keys[5], (PROMPTS, TOKS), 0, 1 << 20) * TOKS + jnp.arange(TOKS, dtype=jnp.int32)[None, :]
    token_order = jnp.argsort(order_keys, axis=1)
    base = jnp.take_along_axis(base, token_order[:, :, None], axis=1)
    replaced = jax.random.randint(keys[6], (PROMPTS, TOKS, 1), 0, replace_of) == 0
    level = jnp.exp(jax.random.uniform(keys[7], (PROMPTS, 1, 1), jnp.float32, jnp.log(level_lo), jnp.log(level_hi)))
    token_value = jnp.where(replaced, fresh, base + level * fresh)
    mixed = 0.8 * token_value + 0.45 * topic[label_list]
    prompt_scale = jnp.exp(jax.random.uniform(keys[8], (PROMPTS, 1, 1), jnp.float32, jnp.log(0.25), jnp.log(2.5)))
    token_scale = jnp.exp(jax.random.uniform(keys[9], (PROMPTS, TOKS, 1), jnp.float32, jnp.log(0.5), jnp.log(2.0)))
    return jnp.clip(0.3 * mixed * prompt_scale * token_scale, -7.0, 7.0).astype(jnp.bfloat16)


def touch_ends(array, rng, smallest, top_value):
    longest = array.shape.index(max(array.shape))
    spots = []
    for shift in (0, 1):
        where = [jax.random.randint(jax.random.fold_in(rng, axis), (), 0, length) for axis, length in enumerate(array.shape)]
        where[longest] = (where[longest] + shift) % array.shape[longest]
        spots.append(tuple(where))
    return array.at[spots[0]].set(smallest).at[spots[1]].set(top_value)


def setup_inputs(seed: int = 0) -> dict:
    key_list = jax.random.split(jax.random.key(seed), 4)
    return {
        "embeds": draw_embeds(jax.random.fold_in(key_list[3], 71), 0),
        "labels": draw_labels(jax.random.fold_in(key_list[3], 71), 0),
        "keep": touch_ends((jax.random.randint(key_list[2], (PROMPTS,), 0, 4) < 3).astype(jnp.int32), jax.random.fold_in(key_list[2], 1), 0, 1),
    }


group_size = 8


def cluster_scores(item):
    member_block, valid_block = item
    total_slots = N_BLK * SLOTS
    everyone = member_block.reshape(total_slots * TOKS, DIM).astype(jnp.float32)
    flags = valid_block.reshape(total_slots)
    groups = member_block.reshape(total_slots // group_size, group_size * TOKS, DIM)
    positions = jnp.arange(total_slots, dtype=jnp.int32).reshape(total_slots // group_size, group_size)
    others = jnp.arange(total_slots, dtype=jnp.int32)

    def one_group(pair):
        queries, query_ids = pair
        score_tile = jnp.dot(queries.astype(jnp.float32), everyone.T, precision=lax.Precision.HIGHEST)
        score_tile = score_tile.reshape(group_size, TOKS, total_slots, TOKS)
        maxsim = jnp.sum(jnp.max(score_tile, axis=3), axis=1) / TOKS
        weights = (query_ids[:, None] != others[None, :]).astype(jnp.float32) * flags[None, :]
        return jnp.sum(maxsim * weights, axis=1), jnp.sum(weights, axis=1)

    sums, counts = lax.map(one_group, (groups, positions))
    sums = sums.reshape(total_slots)
    counts = counts.reshape(total_slots)
    score = jnp.where(flags > 0, sums / jnp.maximum(counts, jnp.float32(1.0)), jnp.float32(0.0))
    return score.reshape(N_BLK, SLOTS)


def reference(embeds, labels, keep):
    shards = N_CLUSTER * N_BLK
    capacity = SLOTS // N_CLUSTER
    tokens = embeds.reshape(shards, P_DEV, TOKS, DIM)
    label_table = labels.reshape(shards, P_DEV).astype(jnp.int32)
    keep_grid = keep.reshape(shards, P_DEV).astype(jnp.float32)
    onehot = (label_table[:, :, None] == jnp.arange(N_CLUSTER, dtype=jnp.int32)[None, None, :]).astype(jnp.int32)
    slot_rank = jnp.sum((jnp.cumsum(onehot, axis=1) - onehot) * onehot, axis=2).astype(jnp.int32)
    shard_ids = jnp.arange(shards, dtype=jnp.int32)
    source_group = (shard_ids // N_BLK)[:, None]
    column = jnp.broadcast_to((shard_ids % N_BLK)[:, None], (shards, P_DEV)).astype(jnp.int32)
    slot_index = (source_group * capacity + slot_rank).astype(jnp.int32)
    members = jnp.zeros((N_CLUSTER, N_BLK, SLOTS, TOKS, DIM), jnp.bfloat16)
    members = members.at[label_table, column, slot_index].set(tokens)
    valid = jnp.zeros((N_CLUSTER, N_BLK, SLOTS), jnp.float32)
    valid = valid.at[label_table, column, slot_index].set(keep_grid)
    scores = lax.map(cluster_scores, (members, valid))
    picked = scores[label_table, column, slot_index] * keep_grid
    return picked.reshape(shards * P_DEV)
```

```python
import functools

import jax
import jax.numpy as jnp
from jax import lax
from jax.experimental import pallas as pl
from jax.experimental.pallas import tpu as pltpu
from jax.sharding import PartitionSpec as P

MESH = pl.DeviceIdType.MESH
NT = (((1,), (1,)), ((), ()))
F32 = jnp.float32
TOKS = 32
SOURCES = 16
CAP = 4
ROWS = TOKS * CAP
P_DEV = 32
LANES = 128

OWN, PARTNER, NEXT, PREV = range(4)


def iota(shape, axis):
    return lax.broadcasted_iota(jnp.int32, shape, axis)


def fold_tokens(tile):
    tile = jnp.maximum(tile, pltpu.roll(tile, 4, 1))
    return jnp.maximum(tile, pltpu.roll(tile, 8, 1))


def pair_block(rows_ref, cols_ref, best_ref, row_sums, lane_sums, first, diagonal):
    both = row_sums is not None
    rows = rows_ref[...].reshape(SOURCES * ROWS, LANES)
    width = 2
    steps = 8 // width
    for step in range(steps):
        tiles = []
        for i in range(width):
            cols = cols_ref[:, pl.ds((step * width + i) * 16, 16), :].reshape(256, LANES)
            tiles.append(lax.dot_general(rows, cols, NT, preferred_element_type=F32))
        for tile in tiles:
            best = jnp.max(tile.reshape(SOURCES, 16, 8, 256), axis=1)
            for c in range(SOURCES):
                piece = jnp.maximum(best[c], pltpu.roll(best[c], 4, 0))
                if diagonal:
                    lane = iota((8, 256), 1)
                    same = (lane // 16 == c) & (lane % 4 == iota((8, 256), 0) % 4)
                    piece = jnp.where(same, 0.0, piece)
                lane_sums = lane_sums + piece
        if both:
            top = functools.reduce(jnp.maximum, tiles)
            if step:
                top = jnp.maximum(top, best_ref[...].reshape(SOURCES * ROWS, 256))
            if step < steps - 1:
                best_ref[...] = top.reshape(SOURCES, ROWS, 256)
            else:
                folded = fold_tokens(top[:, :LANES]) + fold_tokens(top[:, LANES:])
                folded = jnp.sum(folded.reshape(SOURCES, 16, 8, LANES), axis=1)
                row_sums[...] = folded if first else row_sums[...] + folded
    return lane_sums


def kernel(emb, lab_ref, keep_ref, out_ref, outgoing, blocks, best, row_sums, results, returned, count, counts,
           plane_count, plane_counts, send_x, recv_x, send_f, recv_f, send_r, recv_r, send_c, recv_c, send_p, recv_p):
    cl, bk = lax.axis_index("cluster"), lax.axis_index("blk")
    y, core = cl // 4, cl % 2
    x, z = (bk // 4) * 2 + (cl // 2) % 2, bk % 4

    def device(x, y, z, core):
        x, y, z, core = x % 4, y % 4, z % 4, core % 2
        return (y * 4 + (x % 2) * 2 + core, (x // 2) * 4 + z)

    def flip(z):
        return jnp.where(z % 4 == 0, 1, 0)

    def ahead(o):
        return device(x + o // 4, y + o % 4, z, core)

    def column(j):
        return device(x, y, z + 4 - j // 2, core + j)

    readers = {
        NEXT: device(x, y, z + 3, core + flip(z + 3)),
        PREV: device(x, y, z + 1, core + 1 + flip(z)),
        PARTNER: device(x, y, z, core + 1),
    }
    homes = {OWN: (z, core), NEXT: (z + 1, core + flip(z)), PREV: (z + 3, core + 1 + flip(z + 3))}

    barrier = pltpu.get_barrier_semaphore()

    def greet(o, _):
        pl.semaphore_signal(barrier, inc=1, device_id=ahead(o), device_id_type=MESH)
        return 0

    def greet_column(j, _):
        pl.semaphore_signal(barrier, inc=1, device_id=column(j), device_id_type=MESH)
        return 0

    lax.fori_loop(1, SOURCES, greet, 0)
    lax.fori_loop(1, 8, greet_column, 0)

    square = (P_DEV, P_DEV)
    on_diagonal = iota(square, 0) == iota(square, 1)

    def to_col(row):
        return jnp.sum(jnp.where(on_diagonal, jnp.broadcast_to(row, square), 0), axis=1, keepdims=True)

    lab_row, keep_row = lab_ref[...], keep_ref[...]
    lab_col, keep_col = to_col(lab_row), to_col(keep_row)
    equal = jnp.broadcast_to(lab_col, square) == jnp.broadcast_to(lab_row, square)
    rank_row = jnp.sum(jnp.where(equal & (iota(square, 0) < iota(square, 1)), 1, 0), axis=0, keepdims=True)
    rank_col = jnp.sum(jnp.where(equal & (iota(square, 1) < iota(square, 0)), 1, 0), axis=1, keepdims=True)

    def offset(label):
        return (((label >> 2) - x) & 3) * 4 + (((label & 3) - y) & 3)

    slot_row = jnp.where(keep_row > 0, offset(lab_row) * CAP + rank_row, -1).astype(F32)

    wide = P_DEV * 16
    spread = (iota((P_DEV, wide), 1) // 16 == iota((P_DEV, wide), 0)).astype(F32)
    slot_lane = jnp.dot(jnp.broadcast_to(slot_row, (8, P_DEV)).astype(jnp.bfloat16), spread.astype(jnp.bfloat16),
                        preferred_element_type=F32)
    code_lane = slot_lane[0:1].astype(jnp.int32) * 16 + iota((1, wide), 1) % 16
    row = iota((64, wide), 0)
    row_code = (row % 4) * 16 + row // 4
    code_lane = jnp.broadcast_to(code_lane, (64, wide))
    hot = jnp.concatenate(
        [(code_lane == row_code + c * 64).astype(F32).astype(jnp.bfloat16) for c in range(SOURCES)], axis=0)
    tokens = jnp.concatenate(
        [emb[:, pl.ds(h * 16, 16), :].reshape(wide, LANES) for h in range(2)], axis=1)
    picked = jnp.dot(hot, tokens, preferred_element_type=F32).astype(jnp.bfloat16)
    for h in range(2):
        half = picked[:, h * LANES:(h + 1) * LANES].reshape(SOURCES, 64, LANES)
        outgoing[:, pl.ds(h * 64, 64), :] = half
        blocks[OWN, 0, pl.ds(h * 64, 64), :] = half[0]
    labelled = jnp.where(iota((P_DEV, LANES), 1) == lab_col, keep_col.astype(F32), 0.0)
    own_count = jnp.sum(labelled, axis=0, keepdims=True)
    count[...] = own_count

    pl.semaphore_wait(barrier, SOURCES - 1 + 7)

    def dispatch(o):
        return pltpu.make_async_remote_copy(outgoing.at[o], blocks.at[OWN, o], send_x.at[o], recv_x.at[o],
                                            device_id=ahead(o), device_id_type=MESH)

    def tell(o):
        return pltpu.make_async_remote_copy(count, counts.at[o], send_c.at[o], recv_c.at[o],
                                            device_id=ahead(o), device_id_type=MESH)

    def tell_column(j):
        return pltpu.make_async_remote_copy(plane_count, plane_counts.at[j], send_p.at[j], recv_p.at[j],
                                            device_id=column(j), device_id_type=MESH)

    def forward(kind, o):
        return pltpu.make_async_remote_copy(blocks.at[OWN, o], blocks.at[kind, o], send_f.at[kind, o],
                                            recv_f.at[kind, o], device_id=readers[kind], device_id_type=MESH)

    def back(k, kind, o):
        plane, c = homes[kind]
        return pltpu.make_async_remote_copy(results.at[k], returned.at[k, o], send_r.at[k, o], recv_r.at[k, o],
                                            device_id=device(x + 4 - o // 4, y + 4 - o % 4, plane, c),
                                            device_id_type=MESH)

    def each(lo, hi, f):
        def step(i, _):
            f(i)
            return 0
        lax.fori_loop(lo, hi, step, 0)

    each(1, SOURCES, lambda o: dispatch(o).start())
    each(1, SOURCES, lambda o: tell(o).start())

    def pass_on(o):
        for kind in (NEXT, PREV, PARTNER):
            forward(kind, o).start()

    pass_on(0)

    def relay(o):
        dispatch(o).wait_recv()
        pass_on(o)

    each(1, SOURCES, relay)

    each(1, SOURCES, lambda o: tell(o).wait_recv())
    total = own_count
    for o in range(1, SOURCES):
        total = total + counts[o]
    plane_count[...] = total
    each(1, 8, lambda j: tell_column(j).start())

    zero = jnp.zeros((8, 256), F32)
    own = blocks.at[OWN]
    lanes_own = pair_block(own, own, best, None, zero, True, True)
    each(0, SOURCES, lambda o: forward(PARTNER, o).wait_recv())
    lanes_own = pair_block(blocks.at[PARTNER], own, best, None, lanes_own, True, False)
    each(0, SOURCES, lambda o: forward(PREV, o).wait_recv())
    lanes_own = pair_block(blocks.at[PREV], own, best, row_sums.at[1], lanes_own, True, False)
    each(0, SOURCES, lambda o: forward(NEXT, o).wait_recv())
    lanes_own = pair_block(blocks.at[NEXT], own, best, row_sums.at[0], lanes_own, True, False)
    lanes_prev = pair_block(blocks.at[NEXT], blocks.at[PREV], best, row_sums.at[0], zero, False, False)

    into = (256, LANES)
    gather = ((iota(into, 0) // 16 == iota(into, 1) // 8) & (iota(into, 0) % 4 == iota(into, 1) % 8)).astype(F32)

    def from_lanes(sums):
        return jnp.dot(sums * 0.5, gather, preferred_element_type=F32, precision=lax.Precision.HIGHEST)

    kept = ((iota((8, LANES), 1) // 4) % 4 == 3).astype(F32)

    def from_rows(sums):
        return lax.dot_general(kept, sums.reshape(SOURCES * 8, LANES), NT, preferred_element_type=F32,
                               precision=lax.Precision.HIGHEST)

    scale = 1.0 / TOKS
    from_own = jnp.sum(from_lanes(lanes_own), axis=0, keepdims=True) * scale
    results[0] = from_own
    results[1] = from_rows(row_sums[0])[0:1] * scale
    results[2] = (from_rows(row_sums[1])[0:1] + jnp.sum(from_lanes(lanes_prev), axis=0, keepdims=True)) * scale
    each(1, SOURCES, lambda o: back(0, OWN, o).start())
    each(0, SOURCES, lambda o: back(1, NEXT, o).start())
    each(0, SOURCES, lambda o: back(2, PREV, o).start())

    each(1, 8, lambda j: tell_column(j).wait_recv())
    for j in range(1, 8):
        total = total + plane_counts[j]

    each(1, SOURCES, lambda o: back(0, OWN, o).wait_recv())
    each(0, SOURCES, lambda o: back(1, NEXT, o).wait_recv())
    each(0, SOURCES, lambda o: back(2, PREV, o).wait_recv())
    lane = iota((1, LANES), 1)
    scores = jnp.zeros((1, LANES), F32)
    for o in range(SOURCES):
        value = (returned[0, o] if o else from_own) + returned[1, o] + returned[2, o]
        scores = jnp.where(lane // 8 == o, value, scores)

    shape = (P_DEV, LANES)
    lane = iota(shape, 1)
    mine = (lane // 8 == offset(lab_col)) & (lane % 4 == rank_col)
    sums = jnp.sum(jnp.where(mine, jnp.broadcast_to(scores, shape), 0.0), axis=1, keepdims=True)
    members = jnp.sum(jnp.where(lane == lab_col, jnp.broadcast_to(total, shape), 0.0), axis=1, keepdims=True)
    keep = keep_col.astype(F32)
    score = keep * (sums / jnp.maximum(members - keep, 1.0))
    out_ref[...] = jnp.sum(jnp.where(on_diagonal, jnp.broadcast_to(score, square), 0.0), axis=0, keepdims=True)

    each(1, SOURCES, lambda o: dispatch(o).wait_send())
    each(1, SOURCES, lambda o: tell(o).wait_send())
    each(1, 8, lambda j: tell_column(j).wait_send())
    for kind in (NEXT, PREV, PARTNER):
        each(0, SOURCES, lambda o: forward(kind, o).wait_send())
    each(1, SOURCES, lambda o: back(0, OWN, o).wait_send())
    each(0, SOURCES, lambda o: back(1, NEXT, o).wait_send())
    each(0, SOURCES, lambda o: back(2, PREV, o).wait_send())


def body(embeds, labels, keep):
    vmem = pl.BlockSpec(memory_space=pltpu.VMEM)
    dma = pltpu.SemaphoreType.DMA
    bf16 = jnp.bfloat16
    out = pl.pallas_call(
        kernel,
        out_shape=jax.ShapeDtypeStruct((1, P_DEV), F32),
        in_specs=[vmem] * 3,
        out_specs=vmem,
        scratch_shapes=[
            pltpu.VMEM((SOURCES, ROWS, LANES), bf16),
            pltpu.VMEM((4, SOURCES, ROWS, LANES), bf16),
            pltpu.VMEM((SOURCES, ROWS, 256), F32),
            pltpu.VMEM((2, SOURCES, 8, LANES), F32),
            pltpu.VMEM((3, 1, LANES), F32),
            pltpu.VMEM((3, SOURCES, 1, LANES), F32),
            pltpu.VMEM((1, LANES), F32),
            pltpu.VMEM((SOURCES, 1, LANES), F32),
            pltpu.VMEM((1, LANES), F32),
            pltpu.VMEM((8, 1, LANES), F32),
            dma((SOURCES,)), dma((SOURCES,)),
            dma((4, SOURCES)), dma((4, SOURCES)),
            dma((3, SOURCES)), dma((3, SOURCES)),
            dma((SOURCES,)), dma((SOURCES,)),
            dma((8,)), dma((8,)),
        ],
        compiler_params=pltpu.CompilerParams(collective_id=0, has_side_effects=True,
                                             vmem_limit_bytes=48 * 1024 * 1024),
        name="pair_scores",
    )(embeds, labels.reshape(1, P_DEV), keep.reshape(1, P_DEV))
    return out.reshape(P_DEV)


def solution(mesh):
    return jax.shard_map(
        body,
        mesh=mesh,
        in_specs=(
            P(("cluster", "blk"), None, None),
            P(("cluster", "blk"), None),
            P(("cluster", "blk")),
        ),
        out_specs=P(("cluster", "blk")),
        check_vma=False,
    )
```

```python
import functools

import jax
import jax.numpy as jnp
from jax import lax
from jax.experimental import pallas as pl
from jax.experimental.pallas import tpu as pltpu
from jax.sharding import PartitionSpec as P

MESH = pl.DeviceIdType.MESH
NT = (((1,), (1,)), ((), ()))
F32 = jnp.float32
TOKS = 32
SOURCES = 16
CAP = 4
ROWS = TOKS * CAP
P_DEV = 32
LANES = 128

OWN, PARTNER, NEXT, PREV = range(4)

ORDER = ((0, 0), (0, 1), (1, 0), (0, 3), (3, 0), (2, 2), (0, 2), (2, 0), (1, 2), (2, 1), (3, 2), (2, 3), (1, 1), (3, 3),
         (1, 3), (3, 1))
HALF = SOURCES // 2
QUARTER = SOURCES // 4


def packed(values, bits):
    word = sum(v << (bits * i) for i, v in enumerate(values))
    return word - (1 << 32) if word >= 1 << 31 else word


X_OF = packed([o[0] for o in ORDER], 2)
Y_OF = packed([o[1] for o in ORDER], 2)
PLACE = [ORDER.index((i // 4, i % 4)) for i in range(SOURCES)]
PLACE_LO, PLACE_HI = packed(PLACE[:8], 4), packed(PLACE[8:], 4)


def x_of(p):
    return (jnp.int32(X_OF) >> (p * 2)) & 3


def y_of(p):
    return (jnp.int32(Y_OF) >> (p * 2)) & 3


def iota(shape, axis):
    return lax.broadcasted_iota(jnp.int32, shape, axis)


def fold_tokens(tile):
    tile = jnp.maximum(tile, pltpu.roll(tile, 4, 1))
    return jnp.maximum(tile, pltpu.roll(tile, 8, 1))


def pair_block(rows_ref, cols_ref, best_ref, row_sums, lane_sums, first, diagonal=None):
    both = row_sums is not None
    n = rows_ref.shape[0]
    rows = rows_ref[...].reshape(n * ROWS, LANES)
    width = 2
    steps = 8 // width
    for step in range(steps):
        tiles = []
        for i in range(width):
            cols = cols_ref[:, pl.ds((step * width + i) * 16, 16), :].reshape(256, LANES)
            tiles.append(lax.dot_general(rows, cols, NT, preferred_element_type=F32))
        for tile in tiles:
            best = jnp.max(tile.reshape(n, 16, 8, 256), axis=1)
            for c in range(n):
                piece = jnp.maximum(best[c], pltpu.roll(best[c], 4, 0))
                if diagonal is not None:
                    lane = iota((8, 256), 1)
                    same = (lane // 16 == c + diagonal) & (lane % 4 == iota((8, 256), 0) % 4)
                    piece = jnp.where(same, 0.0, piece)
                lane_sums = lane_sums + piece
        if both:
            top = functools.reduce(jnp.maximum, tiles)
            if step:
                top = jnp.maximum(top, best_ref[:n].reshape(n * ROWS, 256))
            if step < steps - 1:
                best_ref[:n] = top.reshape(n, ROWS, 256)
            else:
                folded = fold_tokens(top[:, :LANES]) + fold_tokens(top[:, LANES:])
                folded = jnp.sum(folded.reshape(n, 16, 8, LANES), axis=1)
                row_sums[...] = folded if first else row_sums[...] + folded
    return lane_sums


def kernel(emb_in, lab_in, keep_in, out_ref, emb, lab_ref, keep_ref, outgoing, blocks, best, row_sums, results, inbox,
           returned, count, counts, plane_count, plane_counts, load, send_x, recv_x, send_f, recv_f, send_r, recv_r,
           send_o, recv_o, send_c, recv_c, send_p, recv_p):
    cl, bk = lax.axis_index("cluster"), lax.axis_index("blk")
    y, core = cl // 4, cl % 2
    x, z = (bk // 4) * 2 + (cl // 2) % 2, bk % 4

    def device(x, y, z, core):
        x, y, z, core = x % 4, y % 4, z % 4, core % 2
        return (y * 4 + (x % 2) * 2 + core, (x // 2) * 4 + z)

    def flip(z):
        return jnp.where(z % 4 == 0, 1, 0)

    def ahead(o):
        return device(x + x_of(o), y + y_of(o), z, core)

    def column(j):
        return device(x, y, z + 4 - j // 2, core + j)

    readers = {
        NEXT: device(x, y, z + 3, core + flip(z + 3)),
        PREV: device(x, y, z + 1, core + 1 + flip(z)),
        PARTNER: device(x, y, z, core + 1),
    }
    homes = {PARTNER: (z, core + 1), NEXT: (z + 1, core + flip(z)), PREV: (z + 3, core + 1 + flip(z + 3))}

    barrier = pltpu.get_barrier_semaphore()

    def greet(o, _):
        pl.semaphore_signal(barrier, inc=1, device_id=ahead(o), device_id_type=MESH)
        return 0

    def greet_column(j, _):
        pl.semaphore_signal(barrier, inc=1, device_id=column(j), device_id_type=MESH)
        return 0

    lax.fori_loop(1, SOURCES, greet, 0)
    lax.fori_loop(1, 8, greet_column, 0)

    loads = [pltpu.make_async_copy(src, dst, load.at[i])
             for i, (src, dst) in enumerate(((lab_in, lab_ref), (keep_in, keep_ref), (emb_in, emb)))]
    for item in loads:
        item.start()
    loads[0].wait()
    loads[1].wait()

    square = (P_DEV, P_DEV)
    on_diagonal = iota(square, 0) == iota(square, 1)

    def to_col(row):
        return jnp.sum(jnp.where(on_diagonal, jnp.broadcast_to(row, square), 0), axis=1, keepdims=True)

    lab_row, keep_row = lab_ref[...], keep_ref[...]
    lab_col, keep_col = to_col(lab_row), to_col(keep_row)
    equal = jnp.broadcast_to(lab_col, square) == jnp.broadcast_to(lab_row, square)
    rank_row = jnp.sum(jnp.where(equal & (iota(square, 0) < iota(square, 1)), 1, 0), axis=0, keepdims=True)
    rank_col = jnp.sum(jnp.where(equal & (iota(square, 1) < iota(square, 0)), 1, 0), axis=1, keepdims=True)

    def offset(label):
        o = (((label >> 2) - x) & 3) * 4 + (((label & 3) - y) & 3)
        word = jnp.where(o < 8, jnp.int32(PLACE_LO), jnp.int32(PLACE_HI))
        return (word >> ((o & 7) * 4)) & 15

    slot_row = jnp.where(keep_row > 0, offset(lab_row) * CAP + rank_row, -1).astype(F32)

    wide = P_DEV * 16
    spread = (iota((P_DEV, wide), 1) // 16 == iota((P_DEV, wide), 0)).astype(F32)
    slot_lane = jnp.dot(jnp.broadcast_to(slot_row, (8, P_DEV)).astype(jnp.bfloat16), spread.astype(jnp.bfloat16),
                        preferred_element_type=F32)
    code_lane = slot_lane[0:1].astype(jnp.int32) * 16 + iota((1, wide), 1) % 16
    row = iota((64, wide), 0)
    row_code = (row % 4) * 16 + row // 4
    code_lane = jnp.broadcast_to(code_lane, (64, wide))
    hot = jnp.concatenate(
        [(code_lane == row_code + c * 64).astype(F32).astype(jnp.bfloat16) for c in range(SOURCES)], axis=0)
    loads[2].wait()
    tokens = jnp.concatenate(
        [emb[:, pl.ds(h * 16, 16), :].reshape(wide, LANES) for h in range(2)], axis=1)
    picked = jnp.dot(hot, tokens, preferred_element_type=F32).astype(jnp.bfloat16)
    for h in range(2):
        half = picked[:, h * LANES:(h + 1) * LANES].reshape(SOURCES, 64, LANES)
        outgoing[:, pl.ds(h * 64, 64), :] = half
        blocks[OWN, 0, pl.ds(h * 64, 64), :] = half[0]
    labelled = jnp.where(iota((P_DEV, LANES), 1) == lab_col, keep_col.astype(F32), 0.0)
    own_count = jnp.sum(labelled, axis=0, keepdims=True)
    count[...] = own_count

    pl.semaphore_wait(barrier, SOURCES - 1 + 7)

    def dispatch(o):
        return pltpu.make_async_remote_copy(outgoing.at[o], blocks.at[OWN, o], send_x.at[o], recv_x.at[o],
                                            device_id=ahead(o), device_id_type=MESH)

    def tell(o):
        return pltpu.make_async_remote_copy(count, counts.at[o], send_c.at[o], recv_c.at[o],
                                            device_id=ahead(o), device_id_type=MESH)

    def tell_column(j):
        return pltpu.make_async_remote_copy(plane_count, plane_counts.at[j], send_p.at[j], recv_p.at[j],
                                            device_id=column(j), device_id_type=MESH)

    def forward(kind, o):
        return pltpu.make_async_remote_copy(blocks.at[OWN, o], blocks.at[kind, o], send_f.at[kind, o],
                                            recv_f.at[kind, o], device_id=readers[kind], device_id_type=MESH)

    def hand_over(k):
        plane, c = homes[k]
        return pltpu.make_async_remote_copy(results.at[k], inbox.at[k], send_o.at[k], recv_o.at[k],
                                            device_id=device(x, y, plane, c), device_id_type=MESH)

    def back(o):
        return pltpu.make_async_remote_copy(results.at[OWN], returned.at[o], send_r.at[o], recv_r.at[o],
                                            device_id=device(x + 4 - x_of(o), y + 4 - y_of(o), z, core),
                                            device_id_type=MESH)

    def each(lo, hi, f):
        def step(i, _):
            f(i)
            return 0
        lax.fori_loop(lo, hi, step, 0)

    each(1, SOURCES, lambda o: dispatch(o).start())

    def pass_on(o):
        for kind in (PARTNER, NEXT, PREV):
            forward(kind, o).start()

    pass_on(0)

    each(1, SOURCES, lambda o: tell(o).start())

    def relay(o):
        dispatch(o).wait_recv()
        pass_on(o)

    each(1, SOURCES, relay)

    into = (256, LANES)
    gather = ((iota(into, 0) // 16 == iota(into, 1) // 8) & (iota(into, 0) % 4 == iota(into, 1) % 8)).astype(F32)

    def from_lanes(sums):
        return jnp.dot(sums * 0.5, gather, preferred_element_type=F32, precision=lax.Precision.HIGHEST)

    kept = ((iota((8, LANES), 1) // 4) % 4 == 3).astype(F32)

    def from_rows(sums):
        return lax.dot_general(kept, sums.reshape(SOURCES * 8, LANES), NT, preferred_element_type=F32,
                               precision=lax.Precision.HIGHEST)

    scale = 1.0 / TOKS
    zero = jnp.zeros((8, 256), F32)
    own = blocks.at[OWN]

    lanes_own = pair_block(blocks.at[OWN, :HALF], own, best, None, zero, True, 0)

    each(0, SOURCES, lambda o: forward(PARTNER, o).wait_recv())
    part = pl.ds(core * HALF, HALF)
    row_sums[2] = jnp.zeros((SOURCES, 8, LANES), F32)
    lanes_pair = pair_block(blocks.at[core, part], blocks.at[1 - core], best, row_sums.at[2, part], zero, True)
    by_rows = from_rows(row_sums[2])[0:1] * scale
    by_lanes = jnp.sum(from_lanes(lanes_pair), axis=0, keepdims=True) * scale
    from_pair = jnp.where(core == 0, by_rows, by_lanes)
    results[PARTNER] = jnp.where(core == 0, by_lanes, by_rows)
    hand_over(PARTNER).start()

    each(1, SOURCES, lambda o: tell(o).wait_recv())
    total = own_count
    for o in range(1, SOURCES):
        total = total + counts[o]
    plane_count[...] = total
    each(1, 8, lambda j: tell_column(j).start())

    for q in range(0, SOURCES, QUARTER):
        for kind, k in ((PREV, 1), (NEXT, 0)):
            each(q, q + QUARTER, lambda o, kind=kind: forward(kind, o).wait_recv())
            some = pl.ds(q, QUARTER)
            lanes_own = pair_block(blocks.at[kind, some], own, best, row_sums.at[k, some], lanes_own, True)
    lanes_prev = pair_block(blocks.at[NEXT], blocks.at[PREV], best, row_sums.at[0], zero, False)
    results[NEXT] = from_rows(row_sums[0])[0:1] * scale
    results[PREV] = (from_rows(row_sums[1])[0:1] + jnp.sum(from_lanes(lanes_prev), axis=0, keepdims=True)) * scale
    hand_over(NEXT).start()
    hand_over(PREV).start()

    lanes_own = pair_block(blocks.at[OWN, HALF:], own, best, None, lanes_own, True, HALF)
    from_own = jnp.sum(from_lanes(lanes_own), axis=0, keepdims=True) * scale + from_pair
    for kind in (PARTNER, NEXT, PREV):
        hand_over(kind).wait_recv()
        from_own = from_own + inbox[kind]
    results[OWN] = from_own
    each(1, SOURCES, lambda o: back(o).start())

    each(1, 8, lambda j: tell_column(j).wait_recv())
    for j in range(1, 8):
        total = total + plane_counts[j]

    each(1, SOURCES, lambda o: back(o).wait_recv())
    lane = iota((1, LANES), 1)
    scores = jnp.zeros((1, LANES), F32)
    for o in range(SOURCES):
        scores = jnp.where(lane // 8 == o, returned[o] if o else from_own, scores)

    shape = (P_DEV, LANES)
    lane = iota(shape, 1)
    mine = (lane // 8 == offset(lab_col)) & (lane % 4 == rank_col)
    sums = jnp.sum(jnp.where(mine, jnp.broadcast_to(scores, shape), 0.0), axis=1, keepdims=True)
    members = jnp.sum(jnp.where(lane == lab_col, jnp.broadcast_to(total, shape), 0.0), axis=1, keepdims=True)
    keep = keep_col.astype(F32)
    score = keep * (sums / jnp.maximum(members - keep, 1.0))
    out_ref[...] = jnp.sum(jnp.where(on_diagonal, jnp.broadcast_to(score, square), 0.0), axis=0, keepdims=True)

    each(1, SOURCES, lambda o: dispatch(o).wait_send())
    each(1, SOURCES, lambda o: tell(o).wait_send())
    each(1, 8, lambda j: tell_column(j).wait_send())
    for kind in (PARTNER, NEXT, PREV):
        each(0, SOURCES, lambda o: forward(kind, o).wait_send())
    for kind in (PARTNER, NEXT, PREV):
        hand_over(kind).wait_send()
    each(1, SOURCES, lambda o: back(o).wait_send())


def body(embeds, labels, keep):
    vmem = pl.BlockSpec(memory_space=pltpu.VMEM)
    dma = pltpu.SemaphoreType.DMA
    bf16 = jnp.bfloat16
    out = pl.pallas_call(
        kernel,
        out_shape=jax.ShapeDtypeStruct((1, P_DEV), F32),
        in_specs=[pl.BlockSpec(memory_space=pltpu.HBM)] * 3,
        out_specs=vmem,
        scratch_shapes=[
            pltpu.VMEM((P_DEV, TOKS, LANES), bf16),
            pltpu.VMEM((1, P_DEV), jnp.int32),
            pltpu.VMEM((1, P_DEV), jnp.int32),
            pltpu.VMEM((SOURCES, ROWS, LANES), bf16),
            pltpu.VMEM((4, SOURCES, ROWS, LANES), bf16),
            pltpu.VMEM((SOURCES, ROWS, 256), F32),
            pltpu.VMEM((3, SOURCES, 8, LANES), F32),
            pltpu.VMEM((4, 1, LANES), F32),
            pltpu.VMEM((4, 1, LANES), F32),
            pltpu.VMEM((SOURCES, 1, LANES), F32),
            pltpu.VMEM((1, LANES), F32),
            pltpu.VMEM((SOURCES, 1, LANES), F32),
            pltpu.VMEM((1, LANES), F32),
            pltpu.VMEM((8, 1, LANES), F32),
            dma((3,)),
            dma((SOURCES,)), dma((SOURCES,)),
            dma((4, SOURCES)), dma((4, SOURCES)),
            dma((SOURCES,)), dma((SOURCES,)),
            dma((4,)), dma((4,)),
            dma((SOURCES,)), dma((SOURCES,)),
            dma((8,)), dma((8,)),
        ],
        compiler_params=pltpu.CompilerParams(collective_id=0, has_side_effects=True,
                                             vmem_limit_bytes=48 * 1024 * 1024),
        name="pair_scores",
    )(embeds, labels.reshape(1, P_DEV), keep.reshape(1, P_DEV))
    return out.reshape(P_DEV)


def solution(mesh):
    return jax.shard_map(
        body,
        mesh=mesh,
        in_specs=(
            P(("cluster", "blk"), None, None),
            P(("cluster", "blk"), None),
            P(("cluster", "blk")),
        ),
        out_specs=P(("cluster", "blk")),
        check_vma=False,
    )
```

```python
import functools

import jax
import jax.numpy as jnp
from jax import lax
from jax.experimental import pallas as pl
from jax.experimental.pallas import tpu as pltpu
from jax.sharding import PartitionSpec as P

MESH = pl.DeviceIdType.MESH
NT = (((1,), (1,)), ((), ()))
F32 = jnp.float32
TOKS = 32
SOURCES = 16
CAP = 4
ROWS = TOKS * CAP
P_DEV = 32
LANES = 128

OWN, PARTNER, NEXT, PREV = range(4)

ORDER = ((0, 0), (0, 1), (1, 0), (0, 3), (3, 0), (2, 2), (0, 2), (2, 0), (1, 2), (2, 1), (3, 2), (2, 3), (1, 1), (3, 3),
         (1, 3), (3, 1))
HALF = SOURCES // 2
QUARTER = SOURCES // 2


def packed(values, bits):
    word = sum(v << (bits * i) for i, v in enumerate(values))
    return word - (1 << 32) if word >= 1 << 31 else word


X_OF = packed([o[0] for o in ORDER], 2)
Y_OF = packed([o[1] for o in ORDER], 2)
PLACE = [ORDER.index((i // 4, i % 4)) for i in range(SOURCES)]
PLACE_LO, PLACE_HI = packed(PLACE[:8], 4), packed(PLACE[8:], 4)


def x_of(p):
    return (jnp.int32(X_OF) >> (p * 2)) & 3


def y_of(p):
    return (jnp.int32(Y_OF) >> (p * 2)) & 3


def iota(shape, axis):
    return lax.broadcasted_iota(jnp.int32, shape, axis)


def fold_tokens(tile):
    tile = jnp.maximum(tile, pltpu.roll(tile, 4, 1))
    return jnp.maximum(tile, pltpu.roll(tile, 8, 1))


def pair_block(rows_ref, cols_ref, best_ref, row_sums, lane_sums, first, diagonal=None):
    both = row_sums is not None
    n = rows_ref.shape[0]
    rows = rows_ref[...].reshape(n * ROWS, LANES)
    width = 2
    steps = 8 // width
    for step in range(steps):
        tiles = []
        for i in range(width):
            cols = cols_ref[:, pl.ds((step * width + i) * 16, 16), :].reshape(256, LANES)
            tiles.append(lax.dot_general(rows, cols, NT, preferred_element_type=F32))
        for tile in tiles:
            best = jnp.max(tile.reshape(n, 16, 8, 256), axis=1)
            for c in range(n):
                piece = jnp.maximum(best[c], pltpu.roll(best[c], 4, 0))
                if diagonal is not None:
                    lane = iota((8, 256), 1)
                    same = (lane // 16 == c + diagonal) & (lane % 4 == iota((8, 256), 0) % 4)
                    piece = jnp.where(same, 0.0, piece)
                lane_sums = lane_sums + piece
        if both:
            top = functools.reduce(jnp.maximum, tiles)
            if step:
                top = jnp.maximum(top, best_ref[:n].reshape(n * ROWS, 256))
            if step < steps - 1:
                best_ref[:n] = top.reshape(n, ROWS, 256)
            else:
                folded = fold_tokens(top[:, :LANES]) + fold_tokens(top[:, LANES:])
                folded = jnp.sum(folded.reshape(n, 16, 8, LANES), axis=1)
                row_sums[...] = folded if first else row_sums[...] + folded
    return lane_sums


def kernel(emb_in, lab_in, keep_in, out_ref, emb, lab_ref, keep_ref, outgoing, blocks, best, row_sums, results, inbox,
           returned, count, counts, plane_count, plane_counts, load, send_x, recv_x, send_f, recv_f, send_r, recv_r,
           send_o, recv_o, send_c, recv_c, send_p, recv_p):
    cl, bk = lax.axis_index("cluster"), lax.axis_index("blk")
    y, core = cl // 4, cl % 2
    x, z = (bk // 4) * 2 + (cl // 2) % 2, bk % 4

    def device(x, y, z, core):
        x, y, z, core = x % 4, y % 4, z % 4, core % 2
        return (y * 4 + (x % 2) * 2 + core, (x // 2) * 4 + z)

    def flip(z):
        return jnp.where(z % 4 == 0, 1, 0)

    def ahead(o):
        return device(x + x_of(o), y + y_of(o), z, core)

    def column(j):
        return device(x, y, z + 4 - j // 2, core + j)

    readers = {
        NEXT: device(x, y, z + 3, core + flip(z + 3)),
        PREV: device(x, y, z + 1, core + 1 + flip(z)),
        PARTNER: device(x, y, z, core + 1),
    }
    homes = {PARTNER: (z, core + 1), NEXT: (z + 1, core + flip(z)), PREV: (z + 3, core + 1 + flip(z + 3))}

    barrier = pltpu.get_barrier_semaphore()

    def greet(o, _):
        pl.semaphore_signal(barrier, inc=1, device_id=ahead(o), device_id_type=MESH)
        return 0

    def greet_column(j, _):
        pl.semaphore_signal(barrier, inc=1, device_id=column(j), device_id_type=MESH)
        return 0

    lax.fori_loop(1, SOURCES, greet, 0)
    lax.fori_loop(1, 8, greet_column, 0)

    loads = [pltpu.make_async_copy(src, dst, load.at[i])
             for i, (src, dst) in enumerate(((lab_in, lab_ref), (keep_in, keep_ref), (emb_in, emb)))]
    for item in loads:
        item.start()
    loads[0].wait()
    loads[1].wait()

    square = (P_DEV, P_DEV)
    on_diagonal = iota(square, 0) == iota(square, 1)

    def to_col(row):
        return jnp.sum(jnp.where(on_diagonal, jnp.broadcast_to(row, square), 0), axis=1, keepdims=True)

    lab_row, keep_row = lab_ref[...], keep_ref[...]
    lab_col, keep_col = to_col(lab_row), to_col(keep_row)
    equal = jnp.broadcast_to(lab_col, square) == jnp.broadcast_to(lab_row, square)
    rank_row = jnp.sum(jnp.where(equal & (iota(square, 0) < iota(square, 1)), 1, 0), axis=0, keepdims=True)
    rank_col = jnp.sum(jnp.where(equal & (iota(square, 1) < iota(square, 0)), 1, 0), axis=1, keepdims=True)

    def offset(label):
        o = (((label >> 2) - x) & 3) * 4 + (((label & 3) - y) & 3)
        word = jnp.where(o < 8, jnp.int32(PLACE_LO), jnp.int32(PLACE_HI))
        return (word >> ((o & 7) * 4)) & 15

    slot_row = jnp.where(keep_row > 0, offset(lab_row) * CAP + rank_row, -1).astype(F32)

    wide = P_DEV * 16
    spread = (iota((P_DEV, wide), 1) // 16 == iota((P_DEV, wide), 0)).astype(F32)
    slot_lane = jnp.dot(jnp.broadcast_to(slot_row, (8, P_DEV)).astype(jnp.bfloat16), spread.astype(jnp.bfloat16),
                        preferred_element_type=F32)
    code_lane = slot_lane[0:1].astype(jnp.int32) * 16 + iota((1, wide), 1) % 16
    row = iota((64, wide), 0)
    row_code = (row % 4) * 16 + row // 4
    code_lane = jnp.broadcast_to(code_lane, (64, wide))
    hot = jnp.concatenate(
        [(code_lane == row_code + c * 64).astype(F32).astype(jnp.bfloat16) for c in range(SOURCES)], axis=0)
    loads[2].wait()
    tokens = jnp.concatenate(
        [emb[:, pl.ds(h * 16, 16), :].reshape(wide, LANES) for h in range(2)], axis=1)
    picked = jnp.dot(hot, tokens, preferred_element_type=F32).astype(jnp.bfloat16)
    for h in range(2):
        half = picked[:, h * LANES:(h + 1) * LANES].reshape(SOURCES, 64, LANES)
        outgoing[:, pl.ds(h * 64, 64), :] = half
        blocks[OWN, 0, pl.ds(h * 64, 64), :] = half[0]
    labelled = jnp.where(iota((P_DEV, LANES), 1) == lab_col, keep_col.astype(F32), 0.0)
    own_count = jnp.sum(labelled, axis=0, keepdims=True)
    count[...] = own_count

    pl.semaphore_wait(barrier, SOURCES - 1 + 7)

    def dispatch(o):
        return pltpu.make_async_remote_copy(outgoing.at[o], blocks.at[OWN, o], send_x.at[o], recv_x.at[o],
                                            device_id=ahead(o), device_id_type=MESH)

    def tell(o):
        return pltpu.make_async_remote_copy(count, counts.at[o], send_c.at[o], recv_c.at[o],
                                            device_id=ahead(o), device_id_type=MESH)

    def tell_column(j):
        return pltpu.make_async_remote_copy(plane_count, plane_counts.at[j], send_p.at[j], recv_p.at[j],
                                            device_id=column(j), device_id_type=MESH)

    def forward(kind, o):
        return pltpu.make_async_remote_copy(blocks.at[OWN, o], blocks.at[kind, o], send_f.at[kind, o],
                                            recv_f.at[kind, o], device_id=readers[kind], device_id_type=MESH)

    def hand_over(k):
        plane, c = homes[k]
        return pltpu.make_async_remote_copy(results.at[k], inbox.at[k], send_o.at[k], recv_o.at[k],
                                            device_id=device(x, y, plane, c), device_id_type=MESH)

    def back(o):
        return pltpu.make_async_remote_copy(results.at[OWN], returned.at[o], send_r.at[o], recv_r.at[o],
                                            device_id=device(x + 4 - x_of(o), y + 4 - y_of(o), z, core),
                                            device_id_type=MESH)

    def each(lo, hi, f):
        def step(i, _):
            f(i)
            return 0
        lax.fori_loop(lo, hi, step, 0)

    each(1, SOURCES, lambda o: dispatch(o).start())

    def pass_on(o):
        for kind in (NEXT, PREV, PARTNER):
            forward(kind, o).start()

    pass_on(0)

    each(1, SOURCES, lambda o: tell(o).start())

    def relay(o):
        dispatch(o).wait_recv()
        pass_on(o)

    each(1, SOURCES, relay)

    into = (256, LANES)
    gather = ((iota(into, 0) // 16 == iota(into, 1) // 8) & (iota(into, 0) % 4 == iota(into, 1) % 8)).astype(F32)

    def from_lanes(sums):
        return jnp.dot(sums * 0.5, gather, preferred_element_type=F32, precision=lax.Precision.HIGHEST)

    kept = ((iota((8, LANES), 1) // 4) % 4 == 3).astype(F32)

    def from_rows(sums):
        return lax.dot_general(kept, sums.reshape(SOURCES * 8, LANES), NT, preferred_element_type=F32,
                               precision=lax.Precision.HIGHEST)

    scale = 1.0 / TOKS
    zero = jnp.zeros((8, 256), F32)
    own = blocks.at[OWN]

    lanes_own = pair_block(blocks.at[OWN, :HALF], own, best, None, zero, True, 0)

    each(0, SOURCES, lambda o: forward(PARTNER, o).wait_recv())
    part = pl.ds(core * HALF, HALF)
    row_sums[2] = jnp.zeros((SOURCES, 8, LANES), F32)
    lanes_pair = pair_block(blocks.at[core, part], blocks.at[1 - core], best, row_sums.at[2, part], zero, True)
    by_rows = from_rows(row_sums[2])[0:1] * scale
    by_lanes = jnp.sum(from_lanes(lanes_pair), axis=0, keepdims=True) * scale
    from_pair = jnp.where(core == 0, by_rows, by_lanes)
    results[PARTNER] = jnp.where(core == 0, by_lanes, by_rows)
    hand_over(PARTNER).start()

    each(1, SOURCES, lambda o: tell(o).wait_recv())
    total = own_count
    for o in range(1, SOURCES):
        total = total + counts[o]
    plane_count[...] = total
    each(1, 8, lambda j: tell_column(j).start())

    for q in range(0, SOURCES, QUARTER):
        for kind, k in ((PREV, 1), (NEXT, 0)):
            each(q, q + QUARTER, lambda o, kind=kind: forward(kind, o).wait_recv())
            some = pl.ds(q, QUARTER)
            lanes_own = pair_block(blocks.at[kind, some], own, best, row_sums.at[k, some], lanes_own, True)
    lanes_prev = pair_block(blocks.at[NEXT], blocks.at[PREV], best, row_sums.at[0], zero, False)
    results[NEXT] = from_rows(row_sums[0])[0:1] * scale
    results[PREV] = (from_rows(row_sums[1])[0:1] + jnp.sum(from_lanes(lanes_prev), axis=0, keepdims=True)) * scale
    hand_over(NEXT).start()
    hand_over(PREV).start()

    lanes_own = pair_block(blocks.at[OWN, HALF:], own, best, None, lanes_own, True, HALF)
    from_own = jnp.sum(from_lanes(lanes_own), axis=0, keepdims=True) * scale + from_pair
    for kind in (PARTNER, NEXT, PREV):
        hand_over(kind).wait_recv()
        from_own = from_own + inbox[kind]
    results[OWN] = from_own
    each(1, SOURCES, lambda o: back(o).start())

    each(1, 8, lambda j: tell_column(j).wait_recv())
    for j in range(1, 8):
        total = total + plane_counts[j]

    each(1, SOURCES, lambda o: back(o).wait_recv())
    lane = iota((1, LANES), 1)
    scores = jnp.zeros((1, LANES), F32)
    for o in range(SOURCES):
        scores = jnp.where(lane // 8 == o, returned[o] if o else from_own, scores)

    shape = (P_DEV, LANES)
    lane = iota(shape, 1)
    mine = (lane // 8 == offset(lab_col)) & (lane % 4 == rank_col)
    sums = jnp.sum(jnp.where(mine, jnp.broadcast_to(scores, shape), 0.0), axis=1, keepdims=True)
    members = jnp.sum(jnp.where(lane == lab_col, jnp.broadcast_to(total, shape), 0.0), axis=1, keepdims=True)
    keep = keep_col.astype(F32)
    score = keep * (sums / jnp.maximum(members - keep, 1.0))
    out_ref[...] = jnp.sum(jnp.where(on_diagonal, jnp.broadcast_to(score, square), 0.0), axis=0, keepdims=True)

    each(1, SOURCES, lambda o: dispatch(o).wait_send())
    each(1, SOURCES, lambda o: tell(o).wait_send())
    each(1, 8, lambda j: tell_column(j).wait_send())
    for kind in (PARTNER, NEXT, PREV):
        each(0, SOURCES, lambda o: forward(kind, o).wait_send())
    for kind in (PARTNER, NEXT, PREV):
        hand_over(kind).wait_send()
    each(1, SOURCES, lambda o: back(o).wait_send())


def body(embeds, labels, keep):
    vmem = pl.BlockSpec(memory_space=pltpu.VMEM)
    dma = pltpu.SemaphoreType.DMA
    bf16 = jnp.bfloat16
    out = pl.pallas_call(
        kernel,
        out_shape=jax.ShapeDtypeStruct((1, P_DEV), F32),
        in_specs=[pl.BlockSpec(memory_space=pltpu.HBM)] * 3,
        out_specs=vmem,
        scratch_shapes=[
            pltpu.VMEM((P_DEV, TOKS, LANES), bf16),
            pltpu.VMEM((1, P_DEV), jnp.int32),
            pltpu.VMEM((1, P_DEV), jnp.int32),
            pltpu.VMEM((SOURCES, ROWS, LANES), bf16),
            pltpu.VMEM((4, SOURCES, ROWS, LANES), bf16),
            pltpu.VMEM((SOURCES, ROWS, 256), F32),
            pltpu.VMEM((3, SOURCES, 8, LANES), F32),
            pltpu.VMEM((4, 1, LANES), F32),
            pltpu.VMEM((4, 1, LANES), F32),
            pltpu.VMEM((SOURCES, 1, LANES), F32),
            pltpu.VMEM((1, LANES), F32),
            pltpu.VMEM((SOURCES, 1, LANES), F32),
            pltpu.VMEM((1, LANES), F32),
            pltpu.VMEM((8, 1, LANES), F32),
            dma((3,)),
            dma((SOURCES,)), dma((SOURCES,)),
            dma((4, SOURCES)), dma((4, SOURCES)),
            dma((SOURCES,)), dma((SOURCES,)),
            dma((4,)), dma((4,)),
            dma((SOURCES,)), dma((SOURCES,)),
            dma((8,)), dma((8,)),
        ],
        compiler_params=pltpu.CompilerParams(collective_id=0, has_side_effects=True,
                                             vmem_limit_bytes=48 * 1024 * 1024),
        name="pair_scores",
    )(embeds, labels.reshape(1, P_DEV), keep.reshape(1, P_DEV))
    return out.reshape(P_DEV)


def solution(mesh):
    return jax.shard_map(
        body,
        mesh=mesh,
        in_specs=(
            P(("cluster", "blk"), None, None),
            P(("cluster", "blk"), None),
            P(("cluster", "blk")),
        ),
        out_specs=P(("cluster", "blk")),
        check_vma=False,
    )
```
